128 devices in a mesh: role: 2 (over y_hi), dp: 4 (over y_lo, core), ctx: 16 (over x, z).
Axes of the slice: x: 4, y: 4 (y_hi: 2, y_lo: 2; y = y_hi * 2 + y_lo), z: 4, core: 2. Of those that a mesh axis runs over, the one named last changes fastest.
Arguments:
- teacher_states: bfloat16 [4, 2048, 5120], P('dp', 'ctx'), may hold values from -50 to 50
- student_states: bfloat16 [4, 2048, 3584], P('dp', 'ctx'), may hold values from -50 to 50
- teacher_gain: float32 [5120], replicated, may hold values from 0.25 to 1.75
- student_gain: float32 [3584], replicated, may hold values from 0.25 to 1.75
- mentor_output_weights: bfloat16 [4, 5120, 2048], P(None, None, 'ctx'), may hold values from -2 to 2
- student_heads: bfloat16 [4, 3584, 2048], P(None, None, 'ctx'), may hold values from -2 to 2
- segments: int32 [4, 2048], P('dp', 'ctx'), may hold values from 0 to 31, never falling along the last dimension, each value on 1 to 256 neighbouring positions
- targets: int32 [4, 2048, 4], P('dp', 'ctx'), may hold values from 0 to 2047
Outputs:
- grad_heads: float32 [4, 3584, 2048], P(None, ('role', 'dp'), 'ctx')
- frame_terms: float32 [2, 4, 2048, 4], P('role', 'dp', 'ctx')
The draws below stay inside these ranges and needn't reach their ends.
All inputs are finite; a program needn't handle non-finite values.
Results may differ from the reference program's by a relative error of at most 0.0048.
Values may be sent and summed in bfloat16 or wider, within the bound.
No kernel may reach another device: no remote copies, remote signals or barrier semaphores. Data moves between devices by JAX's collectives and lax.ppermute only.
A program may use at most 192 MiB of HBM per device.

```python
import math
import jax
import jax.numpy as jnp
import numpy as np
from jax import lax

DT = 5120
DS = 3584
CODE_ALPHABET = 2048
QUANTIZER_TOTAL = 4
ROW_DEV = 128
SEQUENCE_STEPS = 2048
DOCS = 32
N_DP = 4


def states_draw(key, seed_tag, model_width):
    values = jnp.clip(jax.random.normal(jax.random.fold_in(key, seed_tag), (N_DP, SEQUENCE_STEPS, model_width), jnp.float32), -5.0, 5.0)
    return values.astype(jnp.bfloat16)


def heads_draw(key, seed_tag, model_width):
    values = jnp.clip(jax.random.normal(jax.random.fold_in(key, seed_tag), (QUANTIZER_TOTAL, model_width, CODE_ALPHABET), jnp.float32), -5.0, 5.0)
    values = values * (3.0 / math.sqrt(model_width))
    return values.astype(jnp.bfloat16)


def draw_teacher_states(key, part):
    return states_draw(key, 11, DT)


def draw_student_states(key, part):
    return states_draw(key, 21, DS)


def draw_mentor_output_weights(key, part):
    return heads_draw(key, 31, DT)


def draw_student_heads(key, part):
    return heads_draw(key, 41, DS)


def place_ends(drawn, stream_key, low, top_value):
    index_at = [jax.random.randint(jax.random.fold_in(stream_key, axis), (), 0, length) for axis, length in enumerate(drawn.shape)]
    widest = drawn.shape.index(max(drawn.shape))
    neighbour = index_at[:widest] + [(index_at[widest] + 1) % drawn.shape[widest]] + index_at[widest + 1:]
    return drawn.at[tuple(index_at)].set(low).at[tuple(neighbour)].set(top_value)


def length_profile(number_of, total, limit, skew):
    weights = [(1 << 20) // math.isqrt(grade ** skew) + 1 for grade in range(2, number_of + 1)]
    rest, holding = total - limit - (number_of - 1), [1] * (number_of - 1)
    while rest > 0:
        free = [i for i in range(number_of - 1) if holding[i] < limit]
        mass, remaining = sum([weights[i] for i in free]), rest
        for i in free:
            addition = min(limit - holding[i], max(1, remaining * weights[i] // mass), rest)
            holding[i] = holding[i] + addition
            rest = rest - addition
    return np.array([limit] + holding)


def ragged(own_key, number_of, total, bound, skew):
    if number_of == 2:
        one = jax.random.randint(own_key, (), max(1, total - bound), min(bound, total - 1) + 1)
        return jnp.stack([one, total - one])
    sizes = jnp.asarray(length_profile(number_of, total, bound, skew), jnp.int32)
    twos = (number_of - 1) // 2
    source_of, receiver = sizes[1:1 + 2 * twos:2], sizes[2:2 + 2 * twos:2]
    slack = jnp.minimum(source_of - 1, bound - receiver)
    moved = jax.random.randint(jax.random.fold_in(own_key, 1), (twos,), 0, 1 << 20) % (slack + 1)
    sizes = sizes.at[1:1 + 2 * twos:2].set(source_of - moved).at[2:2 + 2 * twos:2].set(receiver + moved)
    return sizes[jax.random.permutation(jax.random.fold_in(own_key, 2), number_of)]


def setup_inputs(seed: int = 0) -> dict:
    arg_keys = jax.random.split(jax.random.key(seed), 9)
    return {
        "teacher_states": draw_teacher_states(jax.random.fold_in(arg_keys[8], 71), 0),
        "student_states": draw_student_states(jax.random.fold_in(arg_keys[8], 71), 0),
        "teacher_gain": jnp.clip(1.0 + 0.15 * jax.random.normal(arg_keys[2], (DT,), jnp.float32), 0.25, 1.75),
        "student_gain": jnp.clip(1.0 + 0.15 * jax.random.normal(arg_keys[3], (DS,), jnp.float32), 0.25, 1.75),
        "mentor_output_weights": draw_mentor_output_weights(jax.random.fold_in(arg_keys[8], 71), 0),
        "student_heads": draw_student_heads(jax.random.fold_in(arg_keys[8], 71), 0),
        "segments": jax.vmap(lambda own: jnp.searchsorted(jnp.cumsum(ragged(own, DOCS, SEQUENCE_STEPS, 2 * ROW_DEV, 2)), jnp.arange(SEQUENCE_STEPS), side="right"))(jax.random.split(arg_keys[6], N_DP)).reshape((N_DP, SEQUENCE_STEPS)).astype(jnp.int32),
        "targets": place_ends(jax.random.randint(arg_keys[7], (N_DP, SEQUENCE_STEPS, QUANTIZER_TOTAL), 0, CODE_ALPHABET), jax.random.fold_in(arg_keys[7], 1), 0, CODE_ALPHABET - 1).astype(jnp.int32),
    }


epsilon = 1e-06
sharpness_divisor = 2.0
blend_ratio = 0.5

def normalize(states, gain):
    values = states.astype(jnp.float32)
    factor = lax.rsqrt(lax.optimization_barrier(jnp.mean(values * values, axis=-1, keepdims=True)) + epsilon)
    return (values * factor * gain.astype(jnp.float32)).astype(jnp.bfloat16)

def project_books(rows, heads):
    return jnp.stack([jnp.dot(rows, heads[book], preferred_element_type=jnp.float32) for book in range(QUANTIZER_TOTAL)], axis=1)

def reference(teacher_states, student_states, teacher_gain, student_gain, mentor_output_weights, student_heads, segments, targets):
    teacher_rows = []
    learner_sample_slab = []
    gradient = jnp.zeros((QUANTIZER_TOTAL, DS, CODE_ALPHABET), jnp.float32)
    for sequence in range(N_DP):
        picked_code_index = jax.nn.one_hot(targets[sequence], CODE_ALPHABET, dtype=jnp.float32)
        mentor_unit_scaled = normalize(teacher_states[sequence], teacher_gain)
        mentor_activations = project_books(mentor_unit_scaled, mentor_output_weights) / sharpness_divisor
        teacher_logp = mentor_activations - jax.nn.logsumexp(mentor_activations, axis=-1, keepdims=True)
        teacher_rows.append(-lax.optimization_barrier(jnp.sum(picked_code_index * teacher_logp, axis=-1)))
        teacher_sent = lax.optimization_barrier(teacher_logp.astype(jnp.bfloat16)).astype(jnp.float32)
        student_normed = normalize(student_states[sequence], student_gain)
        learner_activations = project_books(student_normed, student_heads)
        untempered_logdensity = learner_activations - jax.nn.logsumexp(learner_activations, axis=-1, keepdims=True)
        warmed_activations = learner_activations / sharpness_divisor
        warmed_logdensity = warmed_activations - jax.nn.logsumexp(warmed_activations, axis=-1, keepdims=True)
        mentor_distribution = jnp.exp(teacher_sent)
        kullback_gap = lax.optimization_barrier(jnp.sum(mentor_distribution * (teacher_sent - warmed_logdensity), axis=-1))
        mismatch_penalty = -lax.optimization_barrier(jnp.sum(picked_code_index * untempered_logdensity, axis=-1))
        learner_sample_slab.append(blend_ratio * sharpness_divisor * sharpness_divisor * kullback_gap + (1.0 - blend_ratio) * mismatch_penalty)
        members = (segments[sequence][None, :] == jnp.arange(DOCS, dtype=jnp.int32)[:, None]).astype(jnp.float32)
        counts = lax.optimization_barrier(jnp.sum(members, axis=1))
        row_sizes = jnp.dot(counts, members, precision=lax.Precision.HIGHEST)
        sample_importance = SEQUENCE_STEPS / (DOCS * row_sizes)
        gradient_scaling = sample_importance[:, None, None] * (blend_ratio * sharpness_divisor * (jnp.exp(warmed_logdensity) - mentor_distribution) + (1.0 - blend_ratio) * (jnp.exp(untempered_logdensity) - picked_code_index))
        gradient_scaling = gradient_scaling.astype(jnp.bfloat16)
        gradient = gradient + jnp.stack([lax.dot_general(student_normed, gradient_scaling[:, book], (((0,), (0,)), ((), ())), preferred_element_type=jnp.float32) for book in range(QUANTIZER_TOTAL)])
    frame_terms = jnp.stack([jnp.stack(teacher_rows), jnp.stack(learner_sample_slab)])
    return (gradient, frame_terms)
```

```python
import jax
import jax.numpy as jnp
from jax import lax
from jax.sharding import Mesh
from jax.sharding import PartitionSpec as P

BOOKS = 4
SIDE = 4
CTX = ("cx", "cz")
COLUMN = ("role", "ylo")
TURN = ("core", "cx", "cz")

epsilon = 1e-06
sharpness_divisor = 2.0
blend_ratio = 0.5


def line_pairs(phase, step):
    pairs = []
    for core in range(2):
        for x in range(SIDE):
            for z in range(SIDE):
                along_x = (core + phase) % 2 == 0
                to_x = (x + step) % SIDE if along_x else x
                to_z = z if along_x else (z + step) % SIDE
                pairs.append(
                    ((core * SIDE + x) * SIDE + z, (core * SIDE + to_x) * SIDE + to_z)
                )
    return pairs


def moved(value, phase, step):
    return lax.ppermute(value, TURN, line_pairs(phase, step))


def line_blocks(block, phase, way):
    after = moved(block, phase, -1)
    before = moved(block, phase, 1)
    opposite = moved(after, phase, -1) if way > 0 else moved(before, phase, 1)
    return [block, after, opposite, before]


def normalize(states, gain):
    values = states.astype(jnp.float32)
    factor = lax.rsqrt(jnp.mean(values * values, axis=-1, keepdims=True) + epsilon)
    return (values * factor * gain).astype(jnp.bfloat16)


def turned(array, shift, axis):
    double = jnp.concatenate([array, array], axis=axis)
    return lax.dynamic_slice_in_dim(double, shift, array.shape[axis], axis=axis)


def by_place(array, dim):
    mx, mz, core = (lax.axis_index(name) for name in ("cx", "cz", "core"))
    shape = array.shape
    grid = array.reshape(*shape[:dim], SIDE, SIDE, *shape[dim + 1 :])
    grid = turned(turned(grid, mx, dim), mz, dim + 1)
    grid = jnp.where(core == 0, jnp.swapaxes(grid, dim, dim + 1), grid)
    return grid.reshape(shape)


def by_block(array, dim):
    mx, mz, core = (lax.axis_index(name) for name in ("cx", "cz", "core"))
    shape = array.shape
    grid = array.reshape(*shape[:dim], SIDE, SIDE, *shape[dim + 1 :])
    grid = jnp.where(core == 0, jnp.swapaxes(grid, dim, dim + 1), grid)
    grid = turned(turned(grid, (SIDE - mx) % SIDE, dim), (SIDE - mz) % SIDE, dim + 1)
    return grid.reshape(shape)


def copy_for_each(array, axis):
    copies = jnp.broadcast_to(array, (lax.axis_size(axis), *array.shape))
    return lax.all_to_all(copies, axis, split_axis=0, concat_axis=0, tiled=True)


def log_sum(values, axis):
    peak = jnp.max(values, axis=axis, keepdims=True)
    total = jnp.sum(jnp.exp(values - peak), axis=axis, keepdims=True)
    return jnp.squeeze(peak + jnp.log(total), axis)


def on_device(
    teacher_states,
    student_states,
    teacher_gain,
    student_gain,
    mentor_output_weights,
    student_heads,
    segments,
    targets,
):
    columns = student_heads.shape[2]
    features = student_heads.shape[1]
    count = lax.axis_size(CTX)
    role = lax.axis_index("role")
    core = lax.axis_index("core")
    rows_here = teacher_states.shape[1]
    half = rows_here // 2
    length = rows_here * count

    def own_half(states):
        return lax.dynamic_slice_in_dim(states[0], role * half, half, axis=0)

    teacher_rows = normalize(own_half(teacher_states), teacher_gain)
    student_rows = normalize(own_half(student_states), student_gain)

    student_line = jnp.concatenate(line_blocks(student_rows, 0, -1))
    teacher_line = jnp.concatenate(line_blocks(teacher_rows, 0, -1))
    student_parts = line_blocks(student_line, 1, -1)
    teacher_parts = line_blocks(teacher_line, 1, 1)

    info = jnp.concatenate([segments[0][:, None], targets[0]], axis=1)
    info = copy_for_each(info.T, CTX)
    all_segments = info[:, 0].reshape(-1)
    documents = 2 * count
    members = all_segments[:, None] == jnp.arange(documents, dtype=jnp.int32)[None, :]
    members = members.astype(jnp.float32)
    counts = jnp.sum(members, axis=0)
    row_sizes = jnp.sum(members * counts[None, :], axis=1)
    row_weights = length / (documents * row_sizes)

    def half_rows(array):
        pieces = lax.dynamic_slice_in_dim(array, role * half, half, axis=array.ndim - 1)
        return pieces

    weights = by_place(half_rows(row_weights.reshape(count, rows_here)), 0).reshape(-1)
    own_targets = by_place(half_rows(info[:, 1:]), 0)
    own_targets = jnp.moveaxis(own_targets, 1, 0).reshape(BOOKS, -1)
    own_targets = own_targets - lax.axis_index(CTX) * columns
    hits = jnp.arange(columns)[None, None, :] == own_targets[:, :, None]

    def project(rows, heads):
        return jnp.einsum("rd,qdc->qrc", rows, heads, preferred_element_type=jnp.float32)

    teacher_scaled = []
    student_raw = []
    local = []
    for turn in range(SIDE):
        scaled = project(teacher_parts[turn], mentor_output_weights) / sharpness_divisor
        raw = project(student_parts[turn], student_heads)
        teacher_scaled.append(scaled)
        student_raw.append(raw)
        local.append(
            jnp.stack(
                [log_sum(scaled, 2), log_sum(raw, 2), log_sum(raw / sharpness_divisor, 2)]
            )
        )
    scaled = jnp.concatenate(teacher_scaled, axis=1)
    raw = jnp.concatenate(student_raw, axis=1)
    local = jnp.concatenate(local, axis=2)
    sent = by_block(local.reshape(3, BOOKS, count, half), 2)
    whole = log_sum(copy_for_each(sent, CTX), 0)
    whole = by_place(whole, 2).reshape(3, BOOKS, -1)

    teacher_logp = scaled - whole[0][:, :, None]
    plain_logp = raw - whole[1][:, :, None]
    tempered_logp = raw / sharpness_divisor - whole[2][:, :, None]
    teacher_terms = -jnp.sum(jnp.where(hits, teacher_logp, 0.0), axis=2)
    teacher_sent = lax.reduce_precision(teacher_logp, 8, 7)
    teacher_share = jnp.exp(teacher_sent)
    gap = jnp.sum(teacher_share * (teacher_sent - tempered_logp), axis=2)
    mismatch = -jnp.sum(jnp.where(hits, plain_logp, 0.0), axis=2)
    losses = (
        blend_ratio * sharpness_divisor * sharpness_divisor * gap + (1.0 - blend_ratio) * mismatch
    )
    slope = weights[None, :, None] * (
        blend_ratio * sharpness_divisor * (jnp.exp(tempered_logp) - teacher_share)
        + (1.0 - blend_ratio) * (jnp.exp(plain_logp) - hits.astype(jnp.float32))
    )
    slope = slope.astype(jnp.bfloat16)
    student_all = jnp.concatenate(student_parts)
    gradient = jnp.einsum("rd,qrc->qdc", student_all, slope, preferred_element_type=jnp.float32)

    owners = lax.axis_size(COLUMN)
    gradient = gradient.reshape(BOOKS, owners, 2, features // (2 * owners), columns)
    kept = lax.dynamic_index_in_dim(gradient, core, 2, keepdims=False)
    given = lax.dynamic_index_in_dim(gradient, 1 - core, 2, keepdims=False)
    taken = lax.ppermute(given.astype(jnp.bfloat16), "core", [(0, 1), (1, 0)])
    pair = kept + taken.astype(jnp.float32)
    pieces = jnp.moveaxis(pair, 1, 0).astype(jnp.bfloat16)
    pieces = lax.all_to_all(pieces, COLUMN, 0, 0, tiled=True)
    shares = jnp.sum(pieces.astype(jnp.float32), axis=0)

    terms = jnp.stack([teacher_terms, losses]).reshape(2, BOOKS, count, half)
    terms = jnp.moveaxis(by_block(terms, 2), 2, 1)
    terms = lax.all_to_all(
        terms.reshape(2 * count, BOOKS, half), ("role", *CTX), 0, 0, tiled=True
    )
    terms = jnp.sum(terms.reshape(2, count, BOOKS, half), axis=1)
    frame_terms = jnp.moveaxis(terms, 1, 2).reshape(1, 1, rows_here, BOOKS)
    return (shares, frame_terms)


def solution(mesh):
    finer = Mesh(
        mesh.devices.reshape(2, 2, 2, SIDE, SIDE),
        ("role", "ylo", "core", "cx", "cz"),
    )
    dp = ("ylo", "core")
    placed = (
        P(dp, CTX, None),
        P(dp, CTX, None),
        P(),
        P(),
        P(None, None, CTX),
        P(None, None, CTX),
        P(dp, CTX),
        P(dp, CTX, None),
    )
    return jax.shard_map(
        on_device,
        mesh=finer,
        in_specs=placed,
        out_specs=(P(None, ("role", *dp), CTX), P("role", dp, CTX, None)),
        check_vma=False,
    )
```

```python
import functools

import jax
import jax.numpy as jnp
from jax import lax
from jax.experimental import pallas as pl
from jax.experimental.pallas import tpu as pltpu
from jax.sharding import Mesh
from jax.sharding import PartitionSpec as P

BOOKS = 4
SIDE = 4
CTX = ("cx", "cz")
COLUMN = ("role", "ylo")
TURN = ("core", "cx", "cz")

epsilon = 1e-06
sharpness_divisor = 2.0
blend_ratio = 0.5


def line_pairs(phase, step):
    pairs = []
    for core in range(2):
        for x in range(SIDE):
            for z in range(SIDE):
                along_x = (core + phase) % 2 == 0
                to_x = (x + step) % SIDE if along_x else x
                to_z = z if along_x else (z + step) % SIDE
                pairs.append(
                    ((core * SIDE + x) * SIDE + z, (core * SIDE + to_x) * SIDE + to_z)
                )
    return pairs


VMEM = pl.BlockSpec(memory_space=pltpu.VMEM)
SMEM = pl.BlockSpec(memory_space=pltpu.SMEM)


def small_kernel(name, flops=0, transcendentals=0, bytes_accessed=0, limit=8 << 20):
    return {
        "compiler_params": pltpu.CompilerParams(vmem_limit_bytes=limit),
        "cost_estimate": pl.CostEstimate(
            flops=flops, transcendentals=transcendentals, bytes_accessed=bytes_accessed
        ),
        "name": name,
    }


def hold_kernel(array_ref, out_ref, semaphore):
    copy = pltpu.make_async_copy(array_ref, out_ref, semaphore)
    copy.start()
    copy.wait()


def held(array):
    return pl.pallas_call(
        hold_kernel,
        in_specs=[pl.BlockSpec(memory_space=pl.ANY)],
        out_specs=VMEM,
        out_shape=pltpu.VMEM(array.shape, array.dtype),
        scratch_shapes=[pltpu.SemaphoreType.DMA(())],
        **small_kernel("held", bytes_accessed=2 * array.size * array.dtype.itemsize),
    )(array)


def moved(value, phase, step):
    return lax.ppermute(value, TURN, line_pairs(phase, step))


def neighbours(block, phase):
    return moved(block, phase, -1), moved(block, phase, 1)


def normalize(states, gain):
    values = states.astype(jnp.float32)
    factor = lax.rsqrt(jnp.mean(values * values, axis=-1, keepdims=True) + epsilon)
    return (values * factor * gain).astype(jnp.bfloat16)


def joined(pieces, span):
    return jnp.concatenate([piece[:, span] for piece in pieces], axis=0)


def project_kernel(is_teacher, *refs):
    *pieces, heads_ref, out_ref, sums_ref = refs
    features, width = heads_ref.shape[1:]
    depth = features // 4
    for pair in range(BOOKS // 2):
        total = None
        for start in range(0, features, depth):
            span = slice(start, start + depth)
            part = jnp.dot(
                joined(pieces, span),
                jnp.concatenate(
                    [heads_ref[2 * pair, span, :], heads_ref[2 * pair + 1, span, :]], axis=1
                ),
                preferred_element_type=jnp.float32,
            )
            total = part if total is None else total + part
        total = total.T
        if is_teacher:
            total = total / sharpness_divisor
        for side in range(2):
            book = 2 * pair + side
            values = total[side * width : (side + 1) * width]
            out_ref[book] = values
            peak = jnp.max(values, axis=0, keepdims=True)
            found = jnp.sum(jnp.exp(values - peak), axis=0, keepdims=True)
            sums_ref[book : book + 1, :] = peak + jnp.log(found)
            if not is_teacher:
                found = jnp.sum(jnp.exp((values - peak) / sharpness_divisor), axis=0, keepdims=True)
                sums_ref[BOOKS + book : BOOKS + book + 1, :] = (
                    peak / sharpness_divisor + jnp.log(found)
                )


def project(pieces, heads, is_teacher):
    count, features = sum(piece.shape[0] for piece in pieces), pieces[0].shape[1]
    columns = heads.shape[2]
    return pl.pallas_call(
        functools.partial(project_kernel, is_teacher),
        in_specs=[VMEM] * (len(pieces) + 1),
        out_specs=[VMEM, VMEM],
        out_shape=[
            pltpu.VMEM((BOOKS, columns, count), jnp.float32),
            pltpu.VMEM((2 * BOOKS, count), jnp.float32),
        ],
        **small_kernel(
            "project_teacher" if is_teacher else "project_student",
            flops=2 * count * features * BOOKS * columns,
            transcendentals=2 * count * BOOKS * columns,
            bytes_accessed=2 * features * (count + BOOKS * columns) + 4 * count * BOOKS * columns,
        ),
    )(*pieces, heads)


def pack_kernel(place_ref, info_ref, *refs):
    teacher, student = refs[:SIDE], refs[SIDE : 2 * SIDE]
    out_ref, held = refs[2 * SIDE :]
    out_ref[3 * BOOKS] = info_ref[...]
    half = teacher[0].shape[1] // SIDE
    for turn in range(SIDE):
        stacked = jnp.concatenate([teacher[turn][:BOOKS, :], student[turn][...]], axis=0)
        for j in range(SIDE):
            held[turn * SIDE + j] = stacked[:, j * half : (j + 1) * half]
    for pair in range(out_ref.shape[1]):
        first = held[place_ref[2 * pair]]
        second = held[place_ref[2 * pair + 1]]
        out_ref[: 3 * BOOKS, pair, :] = jnp.concatenate([first, second], axis=1)


def pack_sums(place, info, teacher_sums, student_sums):
    half = teacher_sums[0].shape[1] // SIDE
    count = SIDE * SIDE
    return pl.pallas_call(
        pack_kernel,
        in_specs=[SMEM] + [VMEM] * (2 * SIDE + 1),
        out_specs=VMEM,
        out_shape=jax.ShapeDtypeStruct((3 * BOOKS + 1, count // 2, 2 * half), jnp.float32),
        scratch_shapes=[pltpu.VMEM((count, 3 * BOOKS, half), jnp.float32)],
        **small_kernel("pack_sums", bytes_accessed=1 << 17, limit=4 << 20),
    )(place, info, *teacher_sums, *student_sums)


def merged(parts):
    peak = parts[0]
    for part in parts[1:]:
        peak = jnp.maximum(peak, part)
    found = jnp.exp(parts[0] - peak)
    for part in parts[1:]:
        found = found + jnp.exp(part - peak)
    return peak + jnp.log(found)


def merge_kernel(*refs):
    out_ref = refs[-1]
    kinds = 3 * BOOKS
    out_ref[:kinds] = merged([part[:kinds] for part in refs[:-1]])
    for number, part in enumerate(refs[:-1]):
        out_ref[kinds + number] = part[kinds]


def merge_sums(parts):
    return pl.pallas_call(
        merge_kernel,
        in_specs=[VMEM] * len(parts),
        out_specs=VMEM,
        out_shape=jax.ShapeDtypeStruct((3 * BOOKS + SIDE, *parts[0].shape[1:]), jnp.float32),
        **small_kernel("merge_sums", bytes_accessed=1 << 18, limit=4 << 20),
    )(*parts)


def slope_kernel(half, order_ref, *refs):
    arrived, refs = refs[:SIDE], refs[SIDE:]
    teacher, student = refs[:SIDE], refs[SIDE : 2 * SIDE]
    slope_ref, terms_ref, whole, placed, found_terms = refs[2 * SIDE :]
    own_half, first_entry = order_ref[SIDE * SIDE], order_ref[SIDE * SIDE + 1]
    turned_round = order_ref[SIDE * SIDE + 2]
    kinds = 3 * BOOKS
    columns, rows = teacher[0].shape[1], teacher[0].shape[2]
    whole[...] = merged([part[:kinds] for part in arrived])
    segments = jnp.concatenate(
        [
            arrived[dz][kinds + dx, BOOKS : BOOKS + 1, :]
            for dz in range(SIDE)
            for dx in range(SIDE)
        ],
        axis=0,
    )
    documents = 2 * SIDE * SIDE
    length = segments.shape[0] * segments.shape[1]
    sizes = []
    for document in range(documents):
        members = jnp.where(segments == document, 1.0, 0.0)
        sizes.append(jnp.sum(jnp.sum(members, axis=0, keepdims=True), axis=1, keepdims=True))
    for turn in range(SIDE):
        span = slice(turn * rows, (turn + 1) * rows)
        lines, infos = [], []
        for j in range(SIDE):
            block = order_ref[turn * SIDE + j]
            line = whole[:, pl.ds(block // 2, 1), :]
            lines.append(jnp.where(block % 2 == 0, line[:, :, :half], line[:, :, half:]))
            line = jnp.where(
                turned_round == 0, arrived[turn][kinds + j], arrived[j][kinds + turn]
            )
            infos.append(jnp.where(own_half == 0, line[:, :half], line[:, half:]))
        placed[:kinds, :, span] = jnp.concatenate(lines, axis=2)
        info = jnp.concatenate(infos, axis=1)
        segment = info[BOOKS : BOOKS + 1]
        row_sizes = jnp.zeros_like(segment)
        for document in range(documents):
            row_sizes = jnp.where(segment == document, sizes[document], row_sizes)
        placed[kinds, :, span] = length / (documents * row_sizes)
        for each in range(BOOKS):
            placed[kinds + 1 + each, :, span] = info[each : each + 1]

    entries = lax.broadcasted_iota(jnp.int32, (columns, rows), 0)
    for turn in range(SIDE):
        span = slice(turn * rows, (turn + 1) * rows)
        weight = placed[kinds, :, span]
        for book in range(BOOKS):
            target = placed[kinds + 1 + book, :, span].astype(jnp.int32) - first_entry
            raw = student[turn][book]
            teacher_logp = teacher[turn][book] - placed[book, :, span]
            plain_logp = raw - placed[BOOKS + book, :, span]
            tempered_logp = raw / sharpness_divisor - placed[2 * BOOKS + book, :, span]
            hits = entries == target
            teacher_sent = teacher_logp.astype(jnp.bfloat16).astype(jnp.float32)
            share = jnp.exp(teacher_sent)
            gap = jnp.sum(share * (teacher_sent - tempered_logp), axis=0, keepdims=True)
            mismatch = -jnp.sum(jnp.where(hits, plain_logp, 0.0), axis=0, keepdims=True)
            found_terms[book : book + 1, span] = -jnp.sum(
                jnp.where(hits, teacher_logp, 0.0), axis=0, keepdims=True
            )
            found_terms[BOOKS + book : BOOKS + book + 1, span] = (
                blend_ratio * sharpness_divisor * sharpness_divisor * gap
                + (1.0 - blend_ratio) * mismatch
            )
            slope = weight * (
                blend_ratio * sharpness_divisor * (jnp.exp(tempered_logp) - share)
                + (1.0 - blend_ratio) * (jnp.exp(plain_logp) - jnp.where(hits, 1.0, 0.0))
            )
            slope_ref[span, book * columns : (book + 1) * columns] = slope.T.astype(jnp.bfloat16)
    for place in range(SIDE * SIDE):
        lines = found_terms[:, place * half : (place + 1) * half]
        terms_ref[0, order_ref[place]] = lines[:BOOKS]
        terms_ref[1, order_ref[place]] = lines[BOOKS:]


def slopes(order, arrived, teacher_scaled, student_raw, half):
    columns, rows = teacher_scaled[0].shape[1:]
    return pl.pallas_call(
        functools.partial(slope_kernel, half),
        in_specs=[SMEM] + [VMEM] * (3 * SIDE),
        out_specs=[VMEM, VMEM],
        out_shape=[
            pltpu.VMEM((SIDE * rows, BOOKS * columns), jnp.bfloat16),
            jax.ShapeDtypeStruct((2, SIDE * SIDE, BOOKS, half), jnp.float32),
        ],
        scratch_shapes=[
            pltpu.VMEM((3 * BOOKS, *arrived[0].shape[1:]), jnp.float32),
            pltpu.VMEM((4 * BOOKS + 1, 1, SIDE * rows), jnp.float32),
            pltpu.VMEM((2 * BOOKS, SIDE * rows), jnp.float32),
        ],
        **small_kernel(
            "slopes",
            flops=40 * BOOKS * columns * SIDE * rows,
            transcendentals=3 * BOOKS * columns * SIDE * rows,
            bytes_accessed=10 * BOOKS * columns * SIDE * rows,
        ),
    )(order, *arrived, *teacher_scaled, *student_raw)


def flip_kernel(*refs):
    *pieces, out_ref = refs
    width = 512
    for start in range(0, out_ref.shape[0], width):
        span = slice(start, start + width)
        out_ref[span, :] = joined(pieces, span).T


def flipped(pieces):
    count, features = sum(piece.shape[0] for piece in pieces), pieces[0].shape[1]
    return pl.pallas_call(
        flip_kernel,
        in_specs=[VMEM] * len(pieces),
        out_specs=VMEM,
        out_shape=pltpu.VMEM((features, count), pieces[0].dtype),
        **small_kernel("flipped", bytes_accessed=4 * count * features),
    )(*pieces)


def gradient_kernel(with_taken, blocks_ref, *refs):
    rows, slope_ref = refs[:SIDE], refs[SIDE]
    outs = refs[SIDE + 2 if with_taken else SIDE + 1 :]
    step = 0
    for out_ref in outs:
        height = out_ref.shape[1]
        for number in range(out_ref.shape[0]):
            start = pl.multiple_of(blocks_ref[0, step] * height, 64)
            found = jnp.dot(
                jnp.concatenate([part[pl.ds(start, height), :] for part in rows], axis=1),
                slope_ref[...],
                preferred_element_type=jnp.float32,
            )
            if with_taken:
                found = found + refs[SIDE + 1][blocks_ref[1, step]].astype(jnp.float32)
            out_ref[number] = found.astype(out_ref.dtype)
            step += 1


def gradient_blocks(blocks, rows, slope, taken, height, dtype, apart=False):
    count = SIDE * rows[0].shape[1]
    entries = slope.shape[1]
    steps = blocks.shape[1]
    operands = [*rows, slope] + ([] if taken is None else [taken])
    shapes = [(1, height, entries)] * steps if apart else [(steps, height, entries)]
    return pl.pallas_call(
        functools.partial(gradient_kernel, taken is not None),
        in_specs=[SMEM] + [VMEM] * len(operands),
        out_specs=[VMEM] * len(shapes),
        out_shape=[jax.ShapeDtypeStruct(shape, dtype) for shape in shapes],
        **small_kernel(
            "gradient_blocks",
            flops=2 * steps * height * entries * count,
            bytes_accessed=2 * steps * height * (count + entries),
        ),
    )(blocks, *operands)


def total_kernel(own_ref, after_ref, before_ref, opposite_ref, out_ref):
    columns = out_ref.shape[2]
    for book in range(BOOKS):
        span = slice(book * columns, (book + 1) * columns)
        total = own_ref[0, :, span] + after_ref[0, :, span].astype(jnp.float32)
        total = total + before_ref[0, :, span].astype(jnp.float32)
        out_ref[book] = total + opposite_ref[0, :, span].astype(jnp.float32)


def total_of(parts):
    _, height, entries = parts[0].shape
    return pl.pallas_call(
        total_kernel,
        in_specs=[VMEM] * len(parts),
        out_specs=VMEM,
        out_shape=jax.ShapeDtypeStruct((BOOKS, height, entries // BOOKS), jnp.float32),
        **small_kernel("total_of", bytes_accessed=14 * height * entries),
    )(*parts)


def places():
    mx, mz, core = (lax.axis_index(name) for name in ("cx", "cz", "core"))
    place = jnp.arange(SIDE * SIDE, dtype=jnp.int32)
    turn, step = place // SIDE, place % SIDE
    x = (mx + jnp.where(core == 0, step, turn)) % SIDE
    z = (mz + jnp.where(core == 0, turn, step)) % SIDE
    order = (x * SIDE + z).astype(jnp.int32)
    dx, dz = (turn - mx) % SIDE, (step - mz) % SIDE
    return order, jnp.where(core == 0, dz * SIDE + dx, dx * SIDE + dz).astype(jnp.int32)


def on_device(
    teacher_states,
    student_states,
    teacher_gain,
    student_gain,
    mentor_output_weights,
    student_heads,
    segments,
    targets,
):
    columns = student_heads.shape[2]
    features = student_heads.shape[1]
    count = lax.axis_size(CTX)
    role = lax.axis_index("role")
    core = lax.axis_index("core")
    rows_here = teacher_states.shape[1]
    half = rows_here // 2

    def own_half(states):
        return lax.dynamic_slice_in_dim(states[0], role * half, half, axis=0)

    order, place = places()
    order = jnp.concatenate(
        [order, jnp.stack([role, lax.axis_index(CTX) * columns, core]).astype(jnp.int32)]
    )
    owners = lax.axis_size(COLUMN)
    height = features // (2 * owners)
    chip = lax.axis_index(COLUMN)

    def blocks_of(offsets, of_core):
        chips = [(chip + offset) % owners for offset in offsets]
        return jnp.stack(
            [jnp.stack([2 * each + of_core for each in chips]), jnp.array(offsets, jnp.int32)]
        ).astype(jnp.int32)

    away = (2, 1, 3)
    blocks = [
        blocks_of((0,), core),
        blocks_of(away, core),
        blocks_of(range(owners), 1 - core),
    ]

    def back(shift):
        return [(source, (source - shift) % SIDE) for source in range(SIDE)]

    info = jnp.concatenate(
        [targets[0].T, segments, jnp.zeros((BOOKS - 1, rows_here), jnp.int32)]
    ).astype(jnp.float32)
    student_rows = normalize(own_half(student_states), student_gain)
    teacher_rows = normalize(own_half(teacher_states), teacher_gain)
    tie = lax.optimization_barrier
    student_rows, teacher_rows = tie((student_rows, teacher_rows))

    student_near = neighbours(student_rows, 0)
    student_after, student_before, order, place, info, *blocks = tie(
        (*student_near, order, place, info, *blocks)
    )
    student_opposite = moved(student_after, 0, -1)
    teacher_near = neighbours(teacher_rows, 0)
    teacher_after, teacher_before, student_after = tie((*teacher_near, student_after))
    teacher_opposite = moved(teacher_before, 0, 1)
    student_line = jnp.concatenate(
        [student_rows, student_after, student_opposite, student_before]
    )
    student_after, student_before, teacher_opposite = tie(
        (*neighbours(student_line, 1), teacher_opposite)
    )
    teacher_line = jnp.concatenate(
        [teacher_rows, teacher_after, teacher_opposite, teacher_before]
    )
    teacher_after, teacher_before = tie(neighbours(teacher_line, 1))

    def relayed(after, before):
        middle = after.shape[0] // 2
        return (moved(after[:middle], 1, -1), moved(before[middle:], 1, 1))

    student_opposite = relayed(student_after, student_before)
    teacher_opposite = relayed(teacher_after, teacher_before)
    student_parts = [(student_line,), (student_after,), student_opposite, (student_before,)]
    teacher_parts = [(teacher_line,), (teacher_after,), teacher_opposite, (teacher_before,)]
    mentor_output_weights, student_heads = held(mentor_output_weights), held(student_heads)

    def project_teacher(turn):
        return project(teacher_parts[turn], mentor_output_weights, True)

    def project_student(turn):
        return project(student_parts[turn], student_heads, False)

    early = (0, 1, 3)
    flipped_rows = [flipped(student_parts[turn]) for turn in early]
    teacher_found = [project_teacher(turn) for turn in early]
    student_found = [project_student(turn) for turn in early]
    (
        student_parts[2],
        teacher_parts[2],
        flipped_rows,
        teacher_found,
        student_found,
    ) = tie((student_parts[2], teacher_parts[2], flipped_rows, teacher_found, student_found))
    flipped_rows.insert(2, flipped(student_parts[2]))
    student_found.insert(2, project_student(2))
    teacher_found.insert(2, project_teacher(2))
    student_raw, student_sums = zip(*student_found)
    teacher_scaled, teacher_sums = zip(*teacher_found)
    sent = pack_sums(place, info, teacher_sums, student_sums)
    for axis in CTX:
        parts = [
            sent if shift == 0 else lax.ppermute(sent, axis, back(shift)) for shift in range(SIDE)
        ]
        if axis == CTX[0]:
            sent = merge_sums(parts)
    slope, terms = slopes(order, parts, teacher_scaled, student_raw, half)
    (given,) = gradient_blocks(blocks[2], flipped_rows, slope, None, height, jnp.bfloat16)
    taken = lax.ppermute(given, "core", [(0, 1), (1, 0)])
    sent = gradient_blocks(blocks[1], flipped_rows, slope, taken, height, jnp.bfloat16, True)
    slope, *sent = tie((slope, *sent))
    (own,) = gradient_blocks(blocks[0], flipped_rows, slope, taken, height, jnp.float32)
    terms, own = tie((terms, own))
    shares = total_of(
        [own]
        + [
            lax.ppermute(piece, COLUMN, [(y, (y + offset) % owners) for y in range(owners)])
            for offset, piece in zip(away, sent)
        ]
    )

    terms = lax.all_to_all(
        terms.reshape(2 * count, 1, BOOKS * half), ("role", *CTX), 0, 0, tiled=True
    )
    terms = jnp.sum(terms.reshape(2, count, BOOKS, half), axis=1)
    frame_terms = jnp.moveaxis(terms, 1, 2).reshape(1, 1, rows_here, BOOKS)
    return (shares, frame_terms)


def solution(mesh):
    finer = Mesh(
        mesh.devices.reshape(2, 2, 2, SIDE, SIDE),
        ("role", "ylo", "core", "cx", "cz"),
    )
    dp = ("ylo", "core")
    placed = (
        P(dp, CTX, None),
        P(dp, CTX, None),
        P(),
        P(),
        P(None, None, CTX),
        P(None, None, CTX),
        P(dp, CTX),
        P(dp, CTX, None),
    )
    return jax.shard_map(
        on_device,
        mesh=finer,
        in_specs=placed,
        out_specs=(P(None, ("role", *dp), CTX), P("role", dp, CTX, None)),
        check_vma=False,
    )
```

```python
import functools

import jax
import jax.numpy as jnp
from jax import lax
from jax.experimental import pallas as pl
from jax.experimental.pallas import tpu as pltpu
from jax.sharding import Mesh
from jax.sharding import PartitionSpec as P

BOOKS = 4
SIDE = 4
CTX = ("cx", "cz")
COLUMN = ("role", "ylo")
TURN = ("core", "cx", "cz")

epsilon = 1e-06
sharpness_divisor = 2.0
blend_ratio = 0.5


def line_pairs(phase, step):
    pairs = []
    for core in range(2):
        for x in range(SIDE):
            for z in range(SIDE):
                along_x = (core + phase) % 2 == 0
                to_x = (x + step) % SIDE if along_x else x
                to_z = z if along_x else (z + step) % SIDE
                pairs.append(
                    ((core * SIDE + x) * SIDE + z, (core * SIDE + to_x) * SIDE + to_z)
                )
    return pairs


VMEM = pl.BlockSpec(memory_space=pltpu.VMEM)
SMEM = pl.BlockSpec(memory_space=pltpu.SMEM)


def small_kernel(name, flops=0, transcendentals=0, bytes_accessed=0, limit=8 << 20):
    return {
        "compiler_params": pltpu.CompilerParams(vmem_limit_bytes=limit),
        "cost_estimate": pl.CostEstimate(
            flops=flops, transcendentals=transcendentals, bytes_accessed=bytes_accessed
        ),
        "name": name,
    }


def hold_kernel(array_ref, out_ref, semaphore):
    copy = pltpu.make_async_copy(array_ref, out_ref, semaphore)
    copy.start()
    copy.wait()


def held(array):
    return pl.pallas_call(
        hold_kernel,
        in_specs=[pl.BlockSpec(memory_space=pl.ANY)],
        out_specs=VMEM,
        out_shape=pltpu.VMEM(array.shape, array.dtype),
        scratch_shapes=[pltpu.SemaphoreType.DMA(())],
        **small_kernel("held", bytes_accessed=2 * array.size * array.dtype.itemsize),
    )(array)


def moved(value, phase, step):
    return lax.ppermute(value, TURN, line_pairs(phase, step))


def neighbours(block, phase):
    return moved(block, phase, -1), moved(block, phase, 1)


def normalized_kernel(role_ref, *refs):
    for states_ref, gain_ref, out_ref in zip(refs[:2], refs[2:4], refs[4:]):
        values = states_ref[0].astype(jnp.float32)
        factor = lax.rsqrt(jnp.mean(values * values, axis=-1, keepdims=True) + epsilon)
        out_ref[...] = (values * factor * gain_ref[...]).astype(jnp.bfloat16)


def normalized(role, student_states, teacher_states, student_gain, teacher_gain):
    both = (student_states, teacher_states)
    half = student_states.shape[1] // 2
    widths = [states.shape[2] for states in both]
    return pl.pallas_call(
        normalized_kernel,
        grid_spec=pltpu.PrefetchScalarGridSpec(
            num_scalar_prefetch=1,
            grid=(1,),
            in_specs=[
                pl.BlockSpec((1, half, width), lambda step, role: (0, role[0], 0))
                for width in widths
            ]
            + [pl.BlockSpec((1, width), lambda step, role: (0, 0)) for width in widths],
            out_specs=[pl.BlockSpec((half, width), lambda step, role: (0, 0)) for width in widths],
        ),
        out_shape=[jax.ShapeDtypeStruct((half, width), jnp.bfloat16) for width in widths],
        **small_kernel("normalized", bytes_accessed=4 * half * sum(widths), limit=16 << 20),
    )(
        role,
        *(pltpu.with_memory_space_constraint(states, pltpu.HBM) for states in both),
        student_gain[None, :],
        teacher_gain[None, :],
    )


def stack_kernel(*refs):
    *pieces, out_ref = refs
    height = pieces[0].shape[0]
    for number, piece in enumerate(pieces):
        out_ref[number * height : (number + 1) * height, :] = piece[...]


def stacked(pieces):
    height, width = pieces[0].shape
    return pl.pallas_call(
        stack_kernel,
        in_specs=[VMEM] * len(pieces),
        out_specs=VMEM,
        out_shape=pltpu.VMEM((len(pieces) * height, width), pieces[0].dtype),
        **small_kernel("stacked", bytes_accessed=4 * len(pieces) * height * width),
    )(*pieces)


def joined(pieces, span):
    return jnp.concatenate([piece[:, span] for piece in pieces], axis=0)


def project_kernel(is_teacher, *refs):
    *pieces, heads_ref, out_ref, sums_ref = refs
    features, width = heads_ref.shape[1:]
    depth = features // 4
    for pair in range(BOOKS // 2):
        total = None
        for start in range(0, features, depth):
            span = slice(start, start + depth)
            part = jnp.dot(
                joined(pieces, span),
                jnp.concatenate(
                    [heads_ref[2 * pair, span, :], heads_ref[2 * pair + 1, span, :]], axis=1
                ),
                preferred_element_type=jnp.float32,
            )
            total = part if total is None else total + part
        total = total.T
        if is_teacher:
            total = total / sharpness_divisor
        for side in range(2):
            book = 2 * pair + side
            values = total[side * width : (side + 1) * width]
            out_ref[book] = values
            peak = jnp.max(values, axis=0, keepdims=True)
            found = jnp.sum(jnp.exp(values - peak), axis=0, keepdims=True)
            sums_ref[book : book + 1, :] = peak + jnp.log(found)
            if not is_teacher:
                found = jnp.sum(jnp.exp((values - peak) / sharpness_divisor), axis=0, keepdims=True)
                sums_ref[BOOKS + book : BOOKS + book + 1, :] = (
                    peak / sharpness_divisor + jnp.log(found)
                )


def project(pieces, heads, is_teacher):
    count, features = sum(piece.shape[0] for piece in pieces), pieces[0].shape[1]
    columns = heads.shape[2]
    return pl.pallas_call(
        functools.partial(project_kernel, is_teacher),
        in_specs=[VMEM] * (len(pieces) + 1),
        out_specs=[VMEM, VMEM],
        out_shape=[
            pltpu.VMEM((BOOKS, columns, count), jnp.float32),
            pltpu.VMEM((2 * BOOKS, count), jnp.float32),
        ],
        **small_kernel(
            "project_teacher" if is_teacher else "project_student",
            flops=2 * count * features * BOOKS * columns,
            transcendentals=2 * count * BOOKS * columns,
            bytes_accessed=2 * features * (count + BOOKS * columns) + 4 * count * BOOKS * columns,
        ),
    )(*pieces, heads)


def pack_kernel(place_ref, info_ref, *refs):
    teacher, student = refs[:SIDE], refs[SIDE : 2 * SIDE]
    out_ref, held = refs[2 * SIDE :]
    out_ref[3 * BOOKS] = info_ref[...]
    half = teacher[0].shape[1] // SIDE
    for turn in range(SIDE):
        stacked = jnp.concatenate([teacher[turn][:BOOKS, :], student[turn][...]], axis=0)
        for j in range(SIDE):
            held[turn * SIDE + j] = stacked[:, j * half : (j + 1) * half]
    for pair in range(out_ref.shape[1]):
        first = held[place_ref[2 * pair]]
        second = held[place_ref[2 * pair + 1]]
        out_ref[: 3 * BOOKS, pair, :] = jnp.concatenate([first, second], axis=1)


def pack_sums(place, info, teacher_sums, student_sums):
    half = teacher_sums[0].shape[1] // SIDE
    count = SIDE * SIDE
    return pl.pallas_call(
        pack_kernel,
        in_specs=[SMEM] + [VMEM] * (2 * SIDE + 1),
        out_specs=VMEM,
        out_shape=jax.ShapeDtypeStruct((3 * BOOKS + 1, count // 2, 2 * half), jnp.float32),
        scratch_shapes=[pltpu.VMEM((count, 3 * BOOKS, half), jnp.float32)],
        **small_kernel("pack_sums", bytes_accessed=1 << 17, limit=4 << 20),
    )(place, info, *teacher_sums, *student_sums)


def merged(parts):
    peak = parts[0]
    for part in parts[1:]:
        peak = jnp.maximum(peak, part)
    found = jnp.exp(parts[0] - peak)
    for part in parts[1:]:
        found = found + jnp.exp(part - peak)
    return peak + jnp.log(found)


def merge_kernel(*refs):
    out_ref = refs[-1]
    kinds = 3 * BOOKS
    out_ref[:kinds] = merged([part[:kinds] for part in refs[:-1]])
    for number, part in enumerate(refs[:-1]):
        out_ref[kinds + number] = part[kinds]


def merge_sums(parts):
    return pl.pallas_call(
        merge_kernel,
        in_specs=[VMEM] * len(parts),
        out_specs=VMEM,
        out_shape=jax.ShapeDtypeStruct((3 * BOOKS + SIDE, *parts[0].shape[1:]), jnp.float32),
        **small_kernel("merge_sums", bytes_accessed=1 << 18, limit=4 << 20),
    )(*parts)


def slope_kernel(half, order_ref, *refs):
    arrived, refs = refs[:SIDE], refs[SIDE:]
    teacher, student = refs[:SIDE], refs[SIDE : 2 * SIDE]
    slope_ref, terms_ref, whole, placed, found_terms = refs[2 * SIDE :]
    own_half, first_entry = order_ref[SIDE * SIDE], order_ref[SIDE * SIDE + 1]
    turned_round = order_ref[SIDE * SIDE + 2]
    kinds = 3 * BOOKS
    columns, rows = teacher[0].shape[1], teacher[0].shape[2]
    whole[...] = merged([part[:kinds] for part in arrived])
    segments = jnp.concatenate(
        [
            arrived[dz][kinds + dx, BOOKS : BOOKS + 1, :]
            for dz in range(SIDE)
            for dx in range(SIDE)
        ],
        axis=0,
    )
    documents = 2 * SIDE * SIDE
    length = segments.shape[0] * segments.shape[1]
    sizes = []
    for document in range(documents):
        members = jnp.where(segments == document, 1.0, 0.0)
        sizes.append(jnp.sum(jnp.sum(members, axis=0, keepdims=True), axis=1, keepdims=True))
    for turn in range(SIDE):
        span = slice(turn * rows, (turn + 1) * rows)
        lines, infos = [], []
        for j in range(SIDE):
            block = order_ref[turn * SIDE + j]
            line = whole[:, pl.ds(block // 2, 1), :]
            lines.append(jnp.where(block % 2 == 0, line[:, :, :half], line[:, :, half:]))
            line = jnp.where(
                turned_round == 0, arrived[turn][kinds + j], arrived[j][kinds + turn]
            )
            infos.append(jnp.where(own_half == 0, line[:, :half], line[:, half:]))
        placed[:kinds, :, span] = jnp.concatenate(lines, axis=2)
        info = jnp.concatenate(infos, axis=1)
        segment = info[BOOKS : BOOKS + 1]
        row_sizes = jnp.zeros_like(segment)
        for document in range(documents):
            row_sizes = jnp.where(segment == document, sizes[document], row_sizes)
        placed[kinds, :, span] = length / (documents * row_sizes)
        for each in range(BOOKS):
            placed[kinds + 1 + each, :, span] = info[each : each + 1]

    entries = lax.broadcasted_iota(jnp.int32, (columns, rows), 0)
    for turn in range(SIDE):
        span = slice(turn * rows, (turn + 1) * rows)
        weight = placed[kinds, :, span]
        for book in range(BOOKS):
            target = placed[kinds + 1 + book, :, span].astype(jnp.int32) - first_entry
            raw = student[turn][book]
            teacher_logp = teacher[turn][book] - placed[book, :, span]
            plain_logp = raw - placed[BOOKS + book, :, span]
            tempered_logp = raw / sharpness_divisor - placed[2 * BOOKS + book, :, span]
            hits = entries == target
            teacher_sent = teacher_logp.astype(jnp.bfloat16).astype(jnp.float32)
            share = jnp.exp(teacher_sent)
            gap = jnp.sum(share * (teacher_sent - tempered_logp), axis=0, keepdims=True)
            mismatch = -jnp.sum(jnp.where(hits, plain_logp, 0.0), axis=0, keepdims=True)
            found_terms[book : book + 1, span] = -jnp.sum(
                jnp.where(hits, teacher_logp, 0.0), axis=0, keepdims=True
            )
            found_terms[BOOKS + book : BOOKS + book + 1, span] = (
                blend_ratio * sharpness_divisor * sharpness_divisor * gap
                + (1.0 - blend_ratio) * mismatch
            )
            slope = weight * (
                blend_ratio * sharpness_divisor * (jnp.exp(tempered_logp) - share)
                + (1.0 - blend_ratio) * (jnp.exp(plain_logp) - jnp.where(hits, 1.0, 0.0))
            )
            slope_ref[span, book * columns : (book + 1) * columns] = slope.T.astype(jnp.bfloat16)
    for place in range(SIDE * SIDE):
        lines = found_terms[:, place * half : (place + 1) * half]
        terms_ref[0, order_ref[place]] = lines[:BOOKS]
        terms_ref[1, order_ref[place]] = lines[BOOKS:]


def slopes(order, arrived, teacher_scaled, student_raw, half):
    columns, rows = teacher_scaled[0].shape[1:]
    return pl.pallas_call(
        functools.partial(slope_kernel, half),
        in_specs=[SMEM] + [VMEM] * (3 * SIDE),
        out_specs=[VMEM, VMEM],
        out_shape=[
            pltpu.VMEM((SIDE * rows, BOOKS * columns), jnp.bfloat16),
            jax.ShapeDtypeStruct((2, SIDE * SIDE, BOOKS, half), jnp.float32),
        ],
        scratch_shapes=[
            pltpu.VMEM((3 * BOOKS, *arrived[0].shape[1:]), jnp.float32),
            pltpu.VMEM((4 * BOOKS + 1, 1, SIDE * rows), jnp.float32),
            pltpu.VMEM((2 * BOOKS, SIDE * rows), jnp.float32),
        ],
        **small_kernel(
            "slopes",
            flops=40 * BOOKS * columns * SIDE * rows,
            transcendentals=3 * BOOKS * columns * SIDE * rows,
            bytes_accessed=10 * BOOKS * columns * SIDE * rows,
        ),
    )(order, *arrived, *teacher_scaled, *student_raw)


def flip_kernel(*refs):
    *pieces, out_ref = refs
    width = 512
    for start in range(0, out_ref.shape[0], width):
        span = slice(start, start + width)
        out_ref[span, :] = joined(pieces, span).T


def flipped(pieces):
    count, features = sum(piece.shape[0] for piece in pieces), pieces[0].shape[1]
    return pl.pallas_call(
        flip_kernel,
        in_specs=[VMEM] * len(pieces),
        out_specs=VMEM,
        out_shape=pltpu.VMEM((features, count), pieces[0].dtype),
        **small_kernel("flipped", bytes_accessed=4 * count * features),
    )(*pieces)


def gradient_kernel(with_taken, blocks_ref, *refs):
    rows, slope_ref = refs[:SIDE], refs[SIDE]
    outs = refs[SIDE + 2 if with_taken else SIDE + 1 :]
    step = 0
    for out_ref in outs:
        height = out_ref.shape[1]
        for number in range(out_ref.shape[0]):
            start = pl.multiple_of(blocks_ref[0, step] * height, 64)
            found = jnp.dot(
                jnp.concatenate([part[pl.ds(start, height), :] for part in rows], axis=1),
                slope_ref[...],
                preferred_element_type=jnp.float32,
            )
            if with_taken:
                found = found + refs[SIDE + 1][blocks_ref[1, step]].astype(jnp.float32)
            out_ref[number] = found.astype(out_ref.dtype)
            step += 1


def gradient_blocks(blocks, rows, slope, taken, height, dtype, apart=False):
    count = SIDE * rows[0].shape[1]
    entries = slope.shape[1]
    steps = blocks.shape[1]
    operands = [*rows, slope] + ([] if taken is None else [taken])
    shapes = [(1, height, entries)] * steps if apart else [(steps, height, entries)]
    return pl.pallas_call(
        functools.partial(gradient_kernel, taken is not None),
        in_specs=[SMEM] + [VMEM] * len(operands),
        out_specs=[VMEM] * len(shapes),
        out_shape=[jax.ShapeDtypeStruct(shape, dtype) for shape in shapes],
        **small_kernel(
            "gradient_blocks",
            flops=2 * steps * height * entries * count,
            bytes_accessed=2 * steps * height * (count + entries),
        ),
    )(blocks, *operands)


def total_kernel(own_ref, after_ref, before_ref, opposite_ref, out_ref):
    columns = out_ref.shape[2]
    for book in range(BOOKS):
        span = slice(book * columns, (book + 1) * columns)
        total = own_ref[0, :, span] + after_ref[0, :, span].astype(jnp.float32)
        total = total + before_ref[0, :, span].astype(jnp.float32)
        out_ref[book] = total + opposite_ref[0, :, span].astype(jnp.float32)


def total_of(parts):
    _, height, entries = parts[0].shape
    return pl.pallas_call(
        total_kernel,
        in_specs=[VMEM] * len(parts),
        out_specs=VMEM,
        out_shape=jax.ShapeDtypeStruct((BOOKS, height, entries // BOOKS), jnp.float32),
        **small_kernel("total_of", bytes_accessed=14 * height * entries),
    )(*parts)


def places():
    mx, mz, core = (lax.axis_index(name) for name in ("cx", "cz", "core"))
    place = jnp.arange(SIDE * SIDE, dtype=jnp.int32)
    turn, step = place // SIDE, place % SIDE
    x = (mx + jnp.where(core == 0, step, turn)) % SIDE
    z = (mz + jnp.where(core == 0, turn, step)) % SIDE
    order = (x * SIDE + z).astype(jnp.int32)
    dx, dz = (turn - mx) % SIDE, (step - mz) % SIDE
    return order, jnp.where(core == 0, dz * SIDE + dx, dx * SIDE + dz).astype(jnp.int32)


def on_device(
    teacher_states,
    student_states,
    teacher_gain,
    student_gain,
    mentor_output_weights,
    student_heads,
    segments,
    targets,
):
    columns = student_heads.shape[2]
    features = student_heads.shape[1]
    count = lax.axis_size(CTX)
    role = lax.axis_index("role")
    core = lax.axis_index("core")
    rows_here = teacher_states.shape[1]
    half = rows_here // 2

    order, place = places()
    order = jnp.concatenate(
        [order, jnp.stack([role, lax.axis_index(CTX) * columns, core]).astype(jnp.int32)]
    )
    owners = lax.axis_size(COLUMN)
    height = features // (2 * owners)
    chip = lax.axis_index(COLUMN)

    def blocks_of(offsets, of_core):
        chips = [(chip + offset) % owners for offset in offsets]
        return jnp.stack(
            [jnp.stack([2 * each + of_core for each in chips]), jnp.array(offsets, jnp.int32)]
        ).astype(jnp.int32)

    away = (2, 1, 3)
    blocks = [
        blocks_of((0,), core),
        blocks_of(away, core),
        blocks_of(range(owners), 1 - core),
    ]

    def back(shift):
        return [(source, (source - shift) % SIDE) for source in range(SIDE)]

    info = jnp.concatenate(
        [targets[0].T, segments, jnp.zeros((BOOKS - 1, rows_here), jnp.int32)]
    ).astype(jnp.float32)
    student_rows, teacher_rows = normalized(
        role.reshape(1), student_states, teacher_states, student_gain, teacher_gain
    )
    tie = lax.optimization_barrier

    student_near = neighbours(student_rows, 0)
    teacher_after, teacher_before = neighbours(teacher_rows, 0)
    teacher_opposite = moved(teacher_rows, 0, 2)
    student_after, student_before, order, place, info, *blocks = tie(
        (*student_near, order, place, info, *blocks)
    )
    student_opposite = moved(student_after, 0, -1)
    student_line = stacked([student_rows, student_after, student_opposite, student_before])
    teacher_line = stacked([teacher_rows, teacher_after, teacher_opposite, teacher_before])
    teacher_after, teacher_before = tie(neighbours(teacher_line, 1))
    student_after, student_before = tie(neighbours(student_line, 1))

    def relayed(after, before):
        middle = after.shape[0] // 2
        return (moved(after[:middle], 1, -1), moved(before[middle:], 1, 1))

    student_opposite = relayed(student_after, student_before)
    teacher_opposite = relayed(teacher_after, teacher_before)
    student_parts = [(student_line,), (student_after,), student_opposite, (student_before,)]
    teacher_parts = [(teacher_line,), (teacher_after,), teacher_opposite, (teacher_before,)]
    mentor_output_weights, student_heads = held(mentor_output_weights), held(student_heads)

    def project_teacher(turn):
        return project(teacher_parts[turn], mentor_output_weights, True)

    def project_student(turn):
        return project(student_parts[turn], student_heads, False)

    early = (0, 1, 3)
    flipped_rows = [flipped(student_parts[turn]) for turn in early]
    teacher_found = [project_teacher(turn) for turn in early]
    student_found = [project_student(turn) for turn in early]
    teacher_parts[2], flipped_rows, teacher_found, student_found = tie(
        (teacher_parts[2], flipped_rows, teacher_found, student_found)
    )
    teacher_found.insert(2, project_teacher(2))
    teacher_found[2], student_parts[2] = tie((teacher_found[2], student_parts[2]))
    student_found.insert(2, project_student(2))
    flipped_rows.insert(2, flipped(student_parts[2]))
    student_raw, student_sums = zip(*student_found)
    teacher_scaled, teacher_sums = zip(*teacher_found)
    sent = pack_sums(place, info, teacher_sums, student_sums)
    for axis in CTX:
        parts = [
            sent if shift == 0 else lax.ppermute(sent, axis, back(shift)) for shift in range(SIDE)
        ]
        if axis == CTX[0]:
            sent = merge_sums(parts)
    slope, terms = slopes(order, parts, teacher_scaled, student_raw, half)
    (given,) = gradient_blocks(blocks[2], flipped_rows, slope, None, height, jnp.bfloat16)
    taken = lax.ppermute(given, "core", [(0, 1), (1, 0)])
    sent = gradient_blocks(blocks[1], flipped_rows, slope, taken, height, jnp.bfloat16, True)
    slope, *sent = tie((slope, *sent))
    (own,) = gradient_blocks(blocks[0], flipped_rows, slope, taken, height, jnp.float32)
    terms, own = tie((terms, own))
    shares = total_of(
        [own]
        + [
            lax.ppermute(piece, COLUMN, [(y, (y + offset) % owners) for y in range(owners)])
            for offset, piece in zip(away, sent)
        ]
    )

    terms = lax.all_to_all(
        terms.reshape(2 * count, 1, BOOKS * half), ("role", *CTX), 0, 0, tiled=True
    )
    terms = jnp.sum(terms.reshape(2, count, BOOKS, half), axis=1)
    frame_terms = jnp.moveaxis(terms, 1, 2).reshape(1, 1, rows_here, BOOKS)
    return (shares, frame_terms)


def solution(mesh):
    finer = Mesh(
        mesh.devices.reshape(2, 2, 2, SIDE, SIDE),
        ("role", "ylo", "core", "cx", "cz"),
    )
    dp = ("ylo", "core")
    placed = (
        P(dp, CTX, None),
        P(dp, CTX, None),
        P(),
        P(),
        P(None, None, CTX),
        P(None, None, CTX),
        P(dp, CTX),
        P(dp, CTX, None),
    )
    return jax.shard_map(
        on_device,
        mesh=finer,
        in_specs=placed,
        out_specs=(P(None, ("role", *dp), CTX), P("role", dp, CTX, None)),
        check_vma=False,
    )
```

```python
import functools

import jax
import jax.numpy as jnp
from jax import lax
from jax.experimental import pallas as pl
from jax.experimental.pallas import tpu as pltpu
from jax.sharding import Mesh
from jax.sharding import PartitionSpec as P

BOOKS = 4
SIDE = 4
CTX = ("cx", "cz")
COLUMN = ("role", "ylo")
TURN = ("core", "cx", "cz")

epsilon = 1e-06
sharpness_divisor = 2.0
blend_ratio = 0.5


def line_pairs(phase, step):
    pairs = []
    for core in range(2):
        for x in range(SIDE):
            for z in range(SIDE):
                along_x = (core + phase) % 2 == 0
                to_x = (x + step) % SIDE if along_x else x
                to_z = z if along_x else (z + step) % SIDE
                pairs.append(
                    ((core * SIDE + x) * SIDE + z, (core * SIDE + to_x) * SIDE + to_z)
                )
    return pairs


VMEM = pl.BlockSpec(memory_space=pltpu.VMEM)
SMEM = pl.BlockSpec(memory_space=pltpu.SMEM)


def small_kernel(name, flops=0, transcendentals=0, bytes_accessed=0, limit=8 << 20):
    return {
        "compiler_params": pltpu.CompilerParams(vmem_limit_bytes=limit),
        "cost_estimate": pl.CostEstimate(
            flops=flops, transcendentals=transcendentals, bytes_accessed=bytes_accessed
        ),
        "name": name,
    }


def hold_kernel(array_ref, out_ref, semaphore):
    copy = pltpu.make_async_copy(array_ref, out_ref, semaphore)
    copy.start()
    copy.wait()


def held(array):
    return pl.pallas_call(
        hold_kernel,
        in_specs=[pl.BlockSpec(memory_space=pl.ANY)],
        out_specs=VMEM,
        out_shape=pltpu.VMEM(array.shape, array.dtype),
        scratch_shapes=[pltpu.SemaphoreType.DMA(())],
        **small_kernel("held", bytes_accessed=2 * array.size * array.dtype.itemsize),
    )(array)


def moved(value, phase, step):
    return lax.ppermute(value, TURN, line_pairs(phase, step))


def neighbours(block, phase):
    return moved(block, phase, -1), moved(block, phase, 1)


def normalized_kernel(role_ref, *refs):
    for states_ref, gain_ref, out_ref in zip(refs[:2], refs[2:4], refs[4:]):
        values = states_ref[0].astype(jnp.float32)
        factor = lax.rsqrt(jnp.mean(values * values, axis=-1, keepdims=True) + epsilon)
        out_ref[...] = (values * factor * gain_ref[...]).astype(jnp.bfloat16)


def normalized(role, student_states, teacher_states, student_gain, teacher_gain):
    both = (student_states, teacher_states)
    half = student_states.shape[1] // 2
    widths = [states.shape[2] for states in both]
    return pl.pallas_call(
        normalized_kernel,
        grid_spec=pltpu.PrefetchScalarGridSpec(
            num_scalar_prefetch=1,
            grid=(1,),
            in_specs=[
                pl.BlockSpec((1, half, width), lambda step, role: (0, role[0], 0))
                for width in widths
            ]
            + [pl.BlockSpec((1, width), lambda step, role: (0, 0)) for width in widths],
            out_specs=[pl.BlockSpec((half, width), lambda step, role: (0, 0)) for width in widths],
        ),
        out_shape=[jax.ShapeDtypeStruct((half, width), jnp.bfloat16) for width in widths],
        **small_kernel("normalized", bytes_accessed=4 * half * sum(widths), limit=16 << 20),
    )(
        role,
        *(pltpu.with_memory_space_constraint(states, pltpu.HBM) for states in both),
        student_gain[None, :],
        teacher_gain[None, :],
    )


def stack_kernel(*refs):
    *pieces, out_ref = refs
    height = pieces[0].shape[0]
    for number, piece in enumerate(pieces):
        out_ref[number * height : (number + 1) * height, :] = piece[...]


def stacked(pieces):
    height, width = pieces[0].shape
    return pl.pallas_call(
        stack_kernel,
        in_specs=[VMEM] * len(pieces),
        out_specs=VMEM,
        out_shape=pltpu.VMEM((len(pieces) * height, width), pieces[0].dtype),
        **small_kernel("stacked", bytes_accessed=4 * len(pieces) * height * width),
    )(*pieces)


def joined(pieces, span):
    return jnp.concatenate([piece[:, span] for piece in pieces], axis=0)


def project_kernel(is_teacher, *refs):
    *pieces, heads_ref, out_ref, sums_ref = refs
    features, width = heads_ref.shape[1:]
    depth = features // 4
    for pair in range(BOOKS // 2):
        total = None
        for start in range(0, features, depth):
            span = slice(start, start + depth)
            part = jnp.dot(
                joined(pieces, span),
                jnp.concatenate(
                    [heads_ref[2 * pair, span, :], heads_ref[2 * pair + 1, span, :]], axis=1
                ),
                preferred_element_type=jnp.float32,
            )
            total = part if total is None else total + part
        total = total.T
        if is_teacher:
            total = total / sharpness_divisor
        for side in range(2):
            book = 2 * pair + side
            values = total[side * width : (side + 1) * width]
            out_ref[book] = values
            peak = jnp.max(values, axis=0, keepdims=True)
            found = jnp.sum(jnp.exp(values - peak), axis=0, keepdims=True)
            sums_ref[book : book + 1, :] = peak + jnp.log(found)
            if not is_teacher:
                found = jnp.sum(jnp.exp((values - peak) / sharpness_divisor), axis=0, keepdims=True)
                sums_ref[BOOKS + book : BOOKS + book + 1, :] = (
                    peak / sharpness_divisor + jnp.log(found)
                )


def project(pieces, heads, is_teacher):
    count, features = sum(piece.shape[0] for piece in pieces), pieces[0].shape[1]
    columns = heads.shape[2]
    return pl.pallas_call(
        functools.partial(project_kernel, is_teacher),
        in_specs=[VMEM] * (len(pieces) + 1),
        out_specs=[VMEM, VMEM],
        out_shape=[
            pltpu.VMEM((BOOKS, columns, count), jnp.float32),
            pltpu.VMEM((2 * BOOKS, count), jnp.float32),
        ],
        **small_kernel(
            "project_teacher" if is_teacher else "project_student",
            flops=2 * count * features * BOOKS * columns,
            transcendentals=2 * count * BOOKS * columns,
            bytes_accessed=2 * features * (count + BOOKS * columns) + 4 * count * BOOKS * columns,
        ),
    )(*pieces, heads)


def pack_kernel(place_ref, info_ref, *refs):
    teacher, student = refs[:SIDE], refs[SIDE : 2 * SIDE]
    out_ref, held = refs[2 * SIDE :]
    out_ref[3 * BOOKS] = info_ref[...]
    half = teacher[0].shape[1] // SIDE
    for turn in range(SIDE):
        stacked = jnp.concatenate([teacher[turn][:BOOKS, :], student[turn][...]], axis=0)
        for j in range(SIDE):
            held[turn * SIDE + j] = stacked[:, j * half : (j + 1) * half]
    for pair in range(out_ref.shape[1]):
        first = held[place_ref[2 * pair]]
        second = held[place_ref[2 * pair + 1]]
        out_ref[: 3 * BOOKS, pair, :] = jnp.concatenate([first, second], axis=1)


def pack_sums(place, info, teacher_sums, student_sums):
    half = teacher_sums[0].shape[1] // SIDE
    count = SIDE * SIDE
    return pl.pallas_call(
        pack_kernel,
        in_specs=[SMEM] + [VMEM] * (2 * SIDE + 1),
        out_specs=VMEM,
        out_shape=jax.ShapeDtypeStruct((3 * BOOKS + 1, count // 2, 2 * half), jnp.float32),
        scratch_shapes=[pltpu.VMEM((count, 3 * BOOKS, half), jnp.float32)],
        **small_kernel("pack_sums", bytes_accessed=1 << 17, limit=4 << 20),
    )(place, info, *teacher_sums, *student_sums)


def merged(parts):
    peak = parts[0]
    for part in parts[1:]:
        peak = jnp.maximum(peak, part)
    found = jnp.exp(parts[0] - peak)
    for part in parts[1:]:
        found = found + jnp.exp(part - peak)
    return peak + jnp.log(found)


def merge_kernel(*refs):
    out_ref = refs[-1]
    kinds = 3 * BOOKS
    out_ref[:kinds] = merged([part[:kinds] for part in refs[:-1]])
    for number, part in enumerate(refs[:-1]):
        out_ref[kinds + number] = part[kinds]


def merge_sums(parts):
    return pl.pallas_call(
        merge_kernel,
        in_specs=[VMEM] * len(parts),
        out_specs=VMEM,
        out_shape=jax.ShapeDtypeStruct((3 * BOOKS + SIDE, *parts[0].shape[1:]), jnp.float32),
        **small_kernel("merge_sums", bytes_accessed=1 << 18, limit=4 << 20),
    )(*parts)


def slope_kernel(half, order_ref, *refs):
    arrived, refs = refs[:SIDE], refs[SIDE:]
    teacher, student = refs[:SIDE], refs[SIDE : 2 * SIDE]
    slope_ref, terms_ref, whole, placed, found_terms = refs[2 * SIDE :]
    own_half, first_entry = order_ref[SIDE * SIDE], order_ref[SIDE * SIDE + 1]
    turned_round = order_ref[SIDE * SIDE + 2]
    kinds = 3 * BOOKS
    columns, rows = teacher[0].shape[1], teacher[0].shape[2]
    whole[...] = merged([part[:kinds] for part in arrived])
    segments = jnp.concatenate(
        [
            arrived[dz][kinds + dx, BOOKS : BOOKS + 1, :]
            for dz in range(SIDE)
            for dx in range(SIDE)
        ],
        axis=0,
    )
    documents = 2 * SIDE * SIDE
    length = segments.shape[0] * segments.shape[1]
    sizes = []
    for document in range(documents):
        members = jnp.where(segments == document, 1.0, 0.0)
        sizes.append(jnp.sum(jnp.sum(members, axis=0, keepdims=True), axis=1, keepdims=True))
    for turn in range(SIDE):
        span = slice(turn * rows, (turn + 1) * rows)
        lines, infos = [], []
        for j in range(SIDE):
            block = order_ref[turn * SIDE + j]
            line = whole[:, pl.ds(block // 2, 1), :]
            lines.append(jnp.where(block % 2 == 0, line[:, :, :half], line[:, :, half:]))
            line = jnp.where(
                turned_round == 0, arrived[turn][kinds + j], arrived[j][kinds + turn]
            )
            infos.append(jnp.where(own_half == 0, line[:, :half], line[:, half:]))
        placed[:kinds, :, span] = jnp.concatenate(lines, axis=2)
        info = jnp.concatenate(infos, axis=1)
        segment = info[BOOKS : BOOKS + 1]
        row_sizes = jnp.zeros_like(segment)
        for document in range(documents):
            row_sizes = jnp.where(segment == document, sizes[document], row_sizes)
        placed[kinds, :, span] = length / (documents * row_sizes)
        for each in range(BOOKS):
            placed[kinds + 1 + each, :, span] = info[each : each + 1]

    entries = lax.broadcasted_iota(jnp.int32, (columns, rows), 0)
    for turn in range(SIDE):
        span = slice(turn * rows, (turn + 1) * rows)
        weight = placed[kinds, :, span]
        for book in range(BOOKS):
            target = placed[kinds + 1 + book, :, span].astype(jnp.int32) - first_entry
            raw = student[turn][book]
            teacher_logp = teacher[turn][book] - placed[book, :, span]
            plain_logp = raw - placed[BOOKS + book, :, span]
            tempered_logp = raw / sharpness_divisor - placed[2 * BOOKS + book, :, span]
            hits = entries == target
            teacher_sent = teacher_logp.astype(jnp.bfloat16).astype(jnp.float32)
            share = jnp.exp(teacher_sent)
            gap = jnp.sum(share * (teacher_sent - tempered_logp), axis=0, keepdims=True)
            mismatch = -jnp.sum(jnp.where(hits, plain_logp, 0.0), axis=0, keepdims=True)
            found_terms[book : book + 1, span] = -jnp.sum(
                jnp.where(hits, teacher_logp, 0.0), axis=0, keepdims=True
            )
            found_terms[BOOKS + book : BOOKS + book + 1, span] = (
                blend_ratio * sharpness_divisor * sharpness_divisor * gap
                + (1.0 - blend_ratio) * mismatch
            )
            slope = weight * (
                blend_ratio * sharpness_divisor * (jnp.exp(tempered_logp) - share)
                + (1.0 - blend_ratio) * (jnp.exp(plain_logp) - jnp.where(hits, 1.0, 0.0))
            )
            slope_ref[span, book * columns : (book + 1) * columns] = slope.T.astype(jnp.bfloat16)
    for place in range(SIDE * SIDE):
        lines = found_terms[:, place * half : (place + 1) * half]
        terms_ref[0, order_ref[place]] = lines[:BOOKS]
        terms_ref[1, order_ref[place]] = lines[BOOKS:]


def slopes(order, arrived, teacher_scaled, student_raw, half):
    columns, rows = teacher_scaled[0].shape[1:]
    return pl.pallas_call(
        functools.partial(slope_kernel, half),
        in_specs=[SMEM] + [VMEM] * (3 * SIDE),
        out_specs=[VMEM, VMEM],
        out_shape=[
            pltpu.VMEM((SIDE * rows, BOOKS * columns), jnp.bfloat16),
            jax.ShapeDtypeStruct((2, SIDE * SIDE, BOOKS, half), jnp.float32),
        ],
        scratch_shapes=[
            pltpu.VMEM((3 * BOOKS, *arrived[0].shape[1:]), jnp.float32),
            pltpu.VMEM((4 * BOOKS + 1, 1, SIDE * rows), jnp.float32),
            pltpu.VMEM((2 * BOOKS, SIDE * rows), jnp.float32),
        ],
        **small_kernel(
            "slopes",
            flops=40 * BOOKS * columns * SIDE * rows,
            transcendentals=3 * BOOKS * columns * SIDE * rows,
            bytes_accessed=10 * BOOKS * columns * SIDE * rows,
        ),
    )(order, *arrived, *teacher_scaled, *student_raw)


def flip_kernel(*refs):
    *pieces, out_ref = refs
    width = 512
    for start in range(0, out_ref.shape[0], width):
        span = slice(start, start + width)
        out_ref[span, :] = joined(pieces, span).T


def flipped(pieces):
    count, features = sum(piece.shape[0] for piece in pieces), pieces[0].shape[1]
    return pl.pallas_call(
        flip_kernel,
        in_specs=[VMEM] * len(pieces),
        out_specs=VMEM,
        out_shape=pltpu.VMEM((features, count), pieces[0].dtype),
        **small_kernel("flipped", bytes_accessed=4 * count * features),
    )(*pieces)


def gradient_kernel(blocks_ref, *refs):
    *rows, slope_ref, out_ref = refs
    height = out_ref.shape[1]
    for step in range(out_ref.shape[0]):
        start = pl.multiple_of(blocks_ref[0, step] * height, 64)
        found = jnp.dot(
            jnp.concatenate([part[pl.ds(start, height), :] for part in rows], axis=1),
            slope_ref[...],
            preferred_element_type=jnp.float32,
        )
        out_ref[step] = found.astype(out_ref.dtype)


def gradient_blocks(blocks, rows, slope, height, dtype):
    count = SIDE * rows[0].shape[1]
    entries = slope.shape[1]
    steps = blocks.shape[1]
    return pl.pallas_call(
        gradient_kernel,
        in_specs=[SMEM] + [VMEM] * (SIDE + 1),
        out_specs=VMEM,
        out_shape=pltpu.VMEM((steps, height, entries), dtype),
        **small_kernel(
            "gradient_blocks",
            flops=2 * steps * height * entries * count,
            bytes_accessed=2 * steps * height * (count + entries),
        ),
    )(blocks, *rows, slope)


def pair_kernel(order, own_ref, mine_ref, taken_ref, total_ref, *outs):
    total_ref[0] = own_ref[0] + taken_ref[0].astype(jnp.float32)
    for number, (offset, out_ref) in enumerate(zip(order, outs)):
        total = mine_ref[number] + taken_ref[offset].astype(jnp.float32)
        out_ref[0] = total.astype(out_ref.dtype)


def pair_sums(order, own, mine, taken):
    shape = (1, *mine.shape[1:])
    return pl.pallas_call(
        functools.partial(pair_kernel, order),
        in_specs=[VMEM, VMEM, VMEM],
        out_specs=[VMEM] * (len(order) + 1),
        out_shape=[jax.ShapeDtypeStruct(shape, jnp.float32)]
        + [jax.ShapeDtypeStruct(shape, taken.dtype)] * len(order),
        **small_kernel("pair_sums", bytes_accessed=8 * mine.size),
    )(own, mine, taken)


def total_kernel(own_ref, after_ref, before_ref, opposite_ref, out_ref):
    columns = out_ref.shape[2]
    for book in range(BOOKS):
        span = slice(book * columns, (book + 1) * columns)
        total = own_ref[0, :, span] + after_ref[0, :, span].astype(jnp.float32)
        total = total + before_ref[0, :, span].astype(jnp.float32)
        out_ref[book] = total + opposite_ref[0, :, span].astype(jnp.float32)


def total_of(parts):
    _, height, entries = parts[0].shape
    return pl.pallas_call(
        total_kernel,
        in_specs=[VMEM] * len(parts),
        out_specs=VMEM,
        out_shape=jax.ShapeDtypeStruct((BOOKS, height, entries // BOOKS), jnp.float32),
        **small_kernel("total_of", bytes_accessed=14 * height * entries),
    )(*parts)


def places():
    mx, mz, core = (lax.axis_index(name) for name in ("cx", "cz", "core"))
    place = jnp.arange(SIDE * SIDE, dtype=jnp.int32)
    turn, step = place // SIDE, place % SIDE
    x = (mx + jnp.where(core == 0, step, turn)) % SIDE
    z = (mz + jnp.where(core == 0, turn, step)) % SIDE
    order = (x * SIDE + z).astype(jnp.int32)
    dx, dz = (turn - mx) % SIDE, (step - mz) % SIDE
    return order, jnp.where(core == 0, dz * SIDE + dx, dx * SIDE + dz).astype(jnp.int32)


def on_device(
    teacher_states,
    student_states,
    teacher_gain,
    student_gain,
    mentor_output_weights,
    student_heads,
    segments,
    targets,
):
    columns = student_heads.shape[2]
    features = student_heads.shape[1]
    count = lax.axis_size(CTX)
    role = lax.axis_index("role")
    core = lax.axis_index("core")
    rows_here = teacher_states.shape[1]
    half = rows_here // 2

    order, place = places()
    order = jnp.concatenate(
        [order, jnp.stack([role, lax.axis_index(CTX) * columns, core]).astype(jnp.int32)]
    )
    owners = lax.axis_size(COLUMN)
    height = features // (2 * owners)
    chip = lax.axis_index(COLUMN)

    def blocks_of(offsets, of_core):
        chips = [(chip + offset) % owners for offset in offsets]
        return jnp.stack(
            [jnp.stack([2 * each + of_core for each in chips]), jnp.array(offsets, jnp.int32)]
        ).astype(jnp.int32)

    away = (2, 1, 3)
    blocks = [
        blocks_of((0,), core),
        blocks_of(away, core),
        blocks_of(range(owners), 1 - core),
    ]

    def back(shift):
        return [(source, (source - shift) % SIDE) for source in range(SIDE)]

    info = jnp.concatenate(
        [targets[0].T, segments, jnp.zeros((BOOKS - 1, rows_here), jnp.int32)]
    ).astype(jnp.float32)
    student_rows, teacher_rows = normalized(
        role.reshape(1), student_states, teacher_states, student_gain, teacher_gain
    )
    tie = lax.optimization_barrier

    student_near = neighbours(student_rows, 0)
    teacher_after, teacher_before = neighbours(teacher_rows, 0)
    teacher_opposite = moved(teacher_rows, 0, 2)
    student_after, student_before, order, place, info, *blocks = tie(
        (*student_near, order, place, info, *blocks)
    )
    student_opposite = moved(student_after, 0, -1)
    student_line = stacked([student_rows, student_after, student_opposite, student_before])
    teacher_line = stacked([teacher_rows, teacher_after, teacher_opposite, teacher_before])
    teacher_after, teacher_before = tie(neighbours(teacher_line, 1))
    student_after, student_before = tie(neighbours(student_line, 1))

    def relayed(after, before):
        middle = after.shape[0] // 2
        return (moved(after[:middle], 1, -1), moved(before[middle:], 1, 1))

    student_opposite = relayed(student_after, student_before)
    teacher_opposite = relayed(teacher_after, teacher_before)
    student_parts = [(student_line,), (student_after,), student_opposite, (student_before,)]
    teacher_parts = [(teacher_line,), (teacher_after,), teacher_opposite, (teacher_before,)]
    mentor_output_weights, student_heads = held(mentor_output_weights), held(student_heads)

    def project_teacher(turn):
        return project(teacher_parts[turn], mentor_output_weights, True)

    def project_student(turn):
        return project(student_parts[turn], student_heads, False)

    early = (0, 1, 3)
    flipped_rows = [flipped(student_parts[turn]) for turn in early]
    teacher_found = [project_teacher(turn) for turn in early]
    student_found = [project_student(turn) for turn in early]
    teacher_parts[2], flipped_rows, teacher_found, student_found = tie(
        (teacher_parts[2], flipped_rows, teacher_found, student_found)
    )
    teacher_found.insert(2, project_teacher(2))
    teacher_found[2], student_parts[2] = tie((teacher_found[2], student_parts[2]))
    student_found.insert(2, project_student(2))
    flipped_rows.insert(2, flipped(student_parts[2]))
    student_raw, student_sums = zip(*student_found)
    teacher_scaled, teacher_sums = zip(*teacher_found)
    sent = pack_sums(place, info, teacher_sums, student_sums)
    for axis in CTX:
        parts = [
            sent if shift == 0 else lax.ppermute(sent, axis, back(shift)) for shift in range(SIDE)
        ]
        if axis == CTX[0]:
            sent = merge_sums(parts)
    slope, terms = slopes(order, parts, teacher_scaled, student_raw, half)
    given = gradient_blocks(blocks[2], flipped_rows, slope, height, jnp.bfloat16)
    given, slope = tie((given, slope))
    taken = lax.ppermute(given, "core", [(0, 1), (1, 0)])
    mine = gradient_blocks(blocks[1], flipped_rows, slope, height, jnp.float32)
    own = gradient_blocks(blocks[0], flipped_rows, slope, height, jnp.float32)
    own, *sent = pair_sums(away, own, mine, taken)
    terms, own = tie((terms, own))
    shares = total_of(
        [own]
        + [
            lax.ppermute(piece, COLUMN, [(y, (y + offset) % owners) for y in range(owners)])
            for offset, piece in zip(away, sent)
        ]
    )

    terms = lax.all_to_all(
        terms.reshape(2 * count, 1, BOOKS * half), ("role", *CTX), 0, 0, tiled=True
    )
    terms = jnp.sum(terms.reshape(2, count, BOOKS, half), axis=1)
    frame_terms = jnp.moveaxis(terms, 1, 2).reshape(1, 1, rows_here, BOOKS)
    return (shares, frame_terms)


def solution(mesh):
    finer = Mesh(
        mesh.devices.reshape(2, 2, 2, SIDE, SIDE),
        ("role", "ylo", "core", "cx", "cz"),
    )
    dp = ("ylo", "core")
    placed = (
        P(dp, CTX, None),
        P(dp, CTX, None),
        P(),
        P(),
        P(None, None, CTX),
        P(None, None, CTX),
        P(dp, CTX),
        P(dp, CTX, None),
    )
    return jax.shard_map(
        on_device,
        mesh=finer,
        in_specs=placed,
        out_specs=(P(None, ("role", *dp), CTX), P("role", dp, CTX, None)),
        check_vma=False,
    )
```
